32 devices in a mesh: groups: 2 (over y), view: 4 (over z), branch: 2 (over x), mp: 2 (over core).
Axes of the slice: x: 2, y: 2, z: 4, core: 2. Of those that a mesh axis runs over, the one named last changes fastest.
Arguments:
- tokens: bfloat16 [1024, 1024], P(('groups', 'view')), parts along dimension 0, may hold values from -6 to 6
- view_table: bfloat16 [4, 1024], replicated, may hold values from -6 to 6
- view_ids: int32 [8], P('groups'), parts along dimension 0, may hold values from 0 to 3, each once
- view_counts: int32 [8], P('groups'), parts along dimension 0, may hold values from 1 to 128, 384 in all
- norm_in_gain: float32 [1024], replicated, may hold values from 0.1 to 1.9
- in_weight: bfloat16 [1024, 4096], P(None, ('branch', 'mp')), may hold values from -0.1875 to 0.1875
- out_weight: bfloat16 [4096, 1024], P(('branch', 'mp')), may hold values from -0.09375 to 0.09375
- norm_attn_gain: float32 [1024], replicated, may hold values from 0.1 to 1.9
- qkv_weight: bfloat16 [1024, 3, 1024], P(None, None, ('branch', 'mp')), may hold values from -0.1875 to 0.1875
- head_gain: float32 [2, 64], replicated, may hold values from 0.6 to 4
- depth_weight: bfloat16 [1024, 256], P(('branch', 'mp')), may hold values from -0.1875 to 0.1875
- kernel_one: bfloat16 [3, 3, 256, 256], replicated, may hold values from -0.125 to 0.125
- bias_one: float32 [256], replicated, may hold values from -3 to 3
- kernel_two: bfloat16 [3, 3, 256, 256], replicated, may hold values from -0.125 to 0.125
- bias_two: float32 [256], replicated, may hold values from -3 to 3
- track_weight: bfloat16 [1024, 128], P(('branch', 'mp')), may hold values from -0.1875 to 0.1875
- track_ids: int32 [256], P('groups'), parts along dimension 0, may hold values from 0 to 511
Outputs:
- depth_out: bfloat16 [1024, 256], P(('groups', 'view', 'branch', 'mp')), parts along dimension 0
- track_out: float32 [256, 128], P(('groups', 'view', 'branch', 'mp')), parts along dimension 0
The draws below stay inside these ranges and needn't reach their ends.
There are 2 independent parts, one for each index of `groups`. The reference program is written for one: setup_inputs(seed, part) draws one part's arguments, and reference() takes and returns one part's arrays. A program takes and returns all parts, laid end to end along the dimension named above; an argument that names none is the same for every part. Nothing has to cross between parts.
Inputs may be any that keep to these rules, and one draw needn't show every extreme that they name: `view_ids`: each slot names a different view. `view_counts`: some slot is full, with 128 valid tokens; the counts sum to 384.
All inputs are finite; a program needn't handle non-finite values.
Results may differ from the reference program's by a relative error of at most 0.023.
The reference program's roundings to bfloat16 on the way (of `normed_in`, `hidden`, `mlp_out`, `normed_attn`, `weights`, `attended`, `features` and `first_conv`) count: a program that leaves them out, or rounds other values in their place, can miss the bound.
Values may be sent and summed in bfloat16 or wider, within the bound.
No kernel may reach another device: no remote copies, remote signals or barrier semaphores. Data moves between devices by JAX's collectives and lax.ppermute only.
A program may use at most 64 MiB of HBM per device.

```python
import math
import jax
import jax.numpy as jnp
import numpy as np
from jax import lax

D = 1024
FF = 4096
HEADS = 16
HD = 64
CH = 256
TCH = 128
GW = 32
TOK_VIEW = 128
TOKENS = 512
QUERIES = 128
N_VIEW = 4


def draw_head_gain(key, part):
    gain_vals = jnp.exp(jax.random.uniform(key, (2, HD), jnp.float32, math.log(0.6), math.log(2.0)))
    return gain_vals


def set_ends(result, own_key, smallest, largest):
    spot = [jax.random.randint(jax.random.fold_in(own_key, axis), (), 0, length) for axis, length in enumerate(result.shape)]
    widest = result.shape.index(max(result.shape))
    neighbour = spot[:widest] + [(spot[widest] + 1) % result.shape[widest]] + spot[widest + 1:]
    return result.at[tuple(spot)].set(smallest).at[tuple(neighbour)].set(largest)


def block_levels(own_key, dims, pieces, low, top_value):
    loudness, own = 1.0, jax.random.fold_in(own_key, 6)
    for axis_at, parts in pieces:
        draws = jnp.exp(jax.random.uniform(jax.random.fold_in(own, axis_at), (parts,), jnp.float32, low / len(pieces), top_value / len(pieces)))
        loudness = loudness * jnp.repeat(draws, dims[axis_at] // parts).reshape([-1 if axis == axis_at else 1 for axis in range(len(dims))])
    return loudness


def length_profile(amount, total, limit, slope):
    loads = [(1 << 20) // math.isqrt(rank ** slope) + 1 for rank in range(2, amount + 1)]
    rest, holding = total - limit - (amount - 1), [1] * (amount - 1)
    while rest > 0:
        candidates = [i for i in range(amount - 1) if holding[i] < limit]
        whole, remaining = sum([loads[i] for i in candidates]), rest
        for i in candidates:
            addition = min(limit - holding[i], max(1, remaining * loads[i] // whole), rest)
            holding[i] = holding[i] + addition
            rest = rest - addition
    return np.array([limit] + holding)


def uneven_parts(own_key, number_of, total, most, lean):
    if number_of == 2:
        one = jax.random.randint(own_key, (), max(1, total - most), min(most, total - 1) + 1)
        return jnp.stack([one, total - one])
    lengths = jnp.asarray(length_profile(number_of, total, most, lean), jnp.int32)
    twos = (number_of - 1) // 2
    giver, sink = lengths[1:1 + 2 * twos:2], lengths[2:2 + 2 * twos:2]
    margin = jnp.minimum(giver - 1, most - sink)
    shifted = jax.random.randint(jax.random.fold_in(own_key, 1), (twos,), 0, 1 << 20) % (margin + 1)
    lengths = lengths.at[1:1 + 2 * twos:2].set(giver - shifted).at[2:2 + 2 * twos:2].set(sink + shifted)
    return lengths[jax.random.permutation(jax.random.fold_in(own_key, 2), number_of)]


def normal_values(own_key, extent, scale, bound, shards=(), kind=jnp.bfloat16):
    array = jax.random.normal(own_key, extent, jnp.float32) * scale
    if len(shards) > 0:
        array = block_levels(own_key, extent, shards, -0.22, 0.18) * array
    return jnp.clip(array, min=-bound, max=bound).astype(kind)


def setup_inputs(seed: int = 0, part: int = 0) -> dict:
    arg_keys = jax.random.split(jax.random.key(seed), 18)
    part_splits = jax.random.split(jax.random.fold_in(arg_keys[17], part), 18)
    tokens = normal_values(part_splits[0], (TOKENS, D), 1.0, 6.0, ((0, 4),))
    view_table = normal_values(arg_keys[1], (N_VIEW, D), 1.0, 6.0)
    view_ids = jax.random.permutation(part_splits[2], N_VIEW).astype(jnp.int32)
    view_counts = uneven_parts(part_splits[3], N_VIEW, TOK_VIEW * N_VIEW * 3 // 4, TOK_VIEW, 2).astype(jnp.int32)
    norm_in_gain = jnp.clip(1.0 + 0.18 * jax.random.normal(arg_keys[4], (D,), jnp.float32), 0.1, 1.9)
    in_weight = normal_values(arg_keys[5], (D, FF), D ** -0.5, 0.1875, ((1, 4),))
    out_weight = normal_values(arg_keys[6], (FF, D), FF ** -0.5, 0.09375, ((0, 4),))
    norm_attn_gain = jnp.clip(1.0 + 0.18 * jax.random.normal(arg_keys[7], (D,), jnp.float32), 0.1, 1.9)
    qkv_weight = normal_values(arg_keys[8], (D, 3, D), D ** -0.5, 0.1875, ((2, 4),))
    head_gain = draw_head_gain(jax.random.fold_in(arg_keys[17], 71), part)
    depth_weight = normal_values(arg_keys[10], (D, CH), D ** -0.5, 0.1875, ((0, 4),))
    kernel_one = normal_values(arg_keys[11], (3, 3, CH, CH), (9 * CH) ** -0.5, 0.125)
    bias_one = normal_values(arg_keys[12], (CH,), 0.5, 3.0, (), jnp.float32)
    kernel_two = normal_values(arg_keys[13], (3, 3, CH, CH), (9 * CH) ** -0.5, 0.125)
    bias_two = normal_values(arg_keys[14], (CH,), 0.5, 3.0, (), jnp.float32)
    track_weight = normal_values(arg_keys[15], (D, TCH), D ** -0.5, 0.1875, ((0, 4),))
    track_ids = set_ends(jax.random.randint(part_splits[16], (QUERIES,), 0, TOKENS), jax.random.fold_in(part_splits[16], 1), 0, TOKENS - 1).astype(jnp.int32)
    return {"tokens": tokens, "view_table": view_table, "view_ids": view_ids, "view_counts": view_counts, "norm_in_gain": norm_in_gain, "in_weight": in_weight, "out_weight": out_weight, "norm_attn_gain": norm_attn_gain, "qkv_weight": qkv_weight, "head_gain": head_gain, "depth_weight": depth_weight, "kernel_one": kernel_one, "bias_one": bias_one, "kernel_two": kernel_two, "bias_two": bias_two, "track_weight": track_weight, "track_ids": track_ids}


EPS_NORM = 1e-05
EPS_HEAD = 1e-06
NEG_FILL = -1e+30

def layer_norm(values, gain_vec):
    row_mean = lax.optimization_barrier(jnp.mean(values, axis=-1, keepdims=True))
    centered = values - row_mean
    row_var = lax.optimization_barrier(jnp.mean(centered * centered, axis=-1, keepdims=True))
    return centered * lax.rsqrt(row_var + EPS_NORM) * gain_vec

def head_norm(values, gain_vec):
    head_mean = lax.optimization_barrier(jnp.mean(values, axis=-1, keepdims=True))
    centered = values - head_mean
    head_var = lax.optimization_barrier(jnp.mean(centered * centered, axis=-1, keepdims=True))
    return centered * lax.rsqrt(head_var + EPS_HEAD) * gain_vec

def conv_grid(grid_field, kernel, bias_vec):
    num_views, grid_height, grid_width, channels = grid_field.shape
    padded = jnp.pad(grid_field, ((0, 0), (1, 1), (1, 1), (0, 0)))
    running_sum = jnp.zeros((num_views * grid_height * grid_width, kernel.shape[3]), jnp.float32)
    for row_off in range(3):
        for col_off in range(3):
            window = padded[:, row_off:row_off + grid_height, col_off:col_off + grid_width, :].reshape(-1, channels)
            running_sum = running_sum + jnp.dot(window, kernel[row_off, col_off], preferred_element_type=jnp.float32)
    return running_sum + bias_vec

def reference(tokens, view_table, view_ids, view_counts, norm_in_gain, in_weight, out_weight, norm_attn_gain, qkv_weight, head_gain, depth_weight, kernel_one, bias_one, kernel_two, bias_two, track_weight, track_ids):
    view_embed = view_table[view_ids].astype(jnp.float32)
    residual_in = tokens.astype(jnp.float32).reshape(N_VIEW, TOK_VIEW, D) + view_embed[:, None, :]
    residual_in = residual_in.reshape(TOKENS, D)
    normed_in = layer_norm(residual_in, norm_in_gain).astype(jnp.bfloat16)
    hidden = jax.nn.gelu(jnp.dot(normed_in, in_weight, preferred_element_type=jnp.float32), approximate=True).astype(jnp.bfloat16)
    mlp_out = (residual_in + jnp.dot(hidden, out_weight, preferred_element_type=jnp.float32)).astype(jnp.bfloat16)
    normed_attn = layer_norm(mlp_out.astype(jnp.float32), norm_attn_gain).astype(jnp.bfloat16)
    projected = jnp.dot(normed_attn, qkv_weight.reshape(D, 3 * D), preferred_element_type=jnp.float32)
    query_heads = head_norm(projected[:, :D].reshape(TOKENS, HEADS, HD), head_gain[0]).astype(jnp.bfloat16)
    key_heads = head_norm(projected[:, D:2 * D].reshape(TOKENS, HEADS, HD), head_gain[1]).astype(jnp.bfloat16)
    value_heads = projected[:, 2 * D:].reshape(TOKENS, HEADS, HD).astype(jnp.bfloat16)
    positions = jnp.arange(TOKENS, dtype=jnp.int32)
    slot_view = (positions // TOK_VIEW).astype(jnp.int32)
    key_valid = positions % TOK_VIEW < view_counts[slot_view]
    score_scale = 1.0 / HD ** 0.5

    def one_head(operands):
        query_head, key_head, value_head = operands
        scores = jnp.dot(query_head, key_head.T, preferred_element_type=jnp.float32) * score_scale
        scores = jnp.where(key_valid[None, :], scores, NEG_FILL)
        row_max = lax.optimization_barrier(jnp.max(scores, axis=1, keepdims=True))
        weights = jnp.where(key_valid[None, :], jnp.exp(scores - row_max), 0.0)
        row_sum = lax.optimization_barrier(jnp.sum(weights, axis=1, keepdims=True))
        mixed_out = jnp.dot(weights.astype(jnp.bfloat16), value_head, preferred_element_type=jnp.float32)
        return (mixed_out / row_sum).astype(jnp.bfloat16)
    attended = lax.map(one_head, (query_heads.transpose(1, 0, 2), key_heads.transpose(1, 0, 2), value_heads.transpose(1, 0, 2)))
    attended = attended.transpose(1, 0, 2).reshape(TOKENS, D)
    row_valid = key_valid.astype(jnp.float32)[:, None]
    grid_height = TOK_VIEW // GW
    features = (jnp.dot(attended, depth_weight, preferred_element_type=jnp.float32) * row_valid).astype(jnp.bfloat16)
    features = features.reshape(N_VIEW, grid_height, GW, CH)
    first_conv = jnp.maximum(conv_grid(features, kernel_one, bias_one), 0.0).astype(jnp.bfloat16)
    first_conv = first_conv.reshape(N_VIEW, grid_height, GW, CH)
    depth_out = conv_grid(first_conv, kernel_two, bias_two).astype(jnp.bfloat16).reshape(TOKENS, CH)
    picked = attended[track_ids]
    track_out = jnp.dot(picked, track_weight, preferred_element_type=jnp.float32)
    return (depth_out, track_out)
```

```python
import jax
import jax.numpy as jnp
from jax import lax
from jax.sharding import PartitionSpec as P

HD = 64
GW = 32


EPS_NORM = 1e-05
EPS_HEAD = 1e-06
NEG_FILL = -1e30
KEY_BLOCK = 1024


def with_halo(value, sides, width):
    for axis, dim in sides:
        size, length = (lax.axis_size(axis), value.shape[dim])
        up = [(i, (i + 1) % size) for i in range(size - 1)]
        down = [(j, i) for i, j in up]
        last = lax.slice_in_dim(value, length - width, length, axis=dim)
        first = lax.slice_in_dim(value, 0, width, axis=dim)
        before = lax.ppermute(last, axis, up)
        after = lax.ppermute(first, axis, down)
        value = jnp.concatenate([before, value, after], axis=dim)
    return value


def layer_norm(values, gain_vec):
    row_mean = jnp.mean(values, axis=-1, keepdims=True)
    centered = values - row_mean
    row_var = jnp.mean(centered * centered, axis=-1, keepdims=True)
    return centered * lax.rsqrt(row_var + EPS_NORM) * gain_vec


def head_norm(values, gain_vec):
    head_mean = jnp.mean(values, axis=-1, keepdims=True)
    centered = values - head_mean
    head_var = jnp.mean(centered * centered, axis=-1, keepdims=True)
    return centered * lax.rsqrt(head_var + EPS_HEAD) * gain_vec


def conv_rows(grid_field, kernel, bias_vec):
    extended = with_halo(grid_field, ((("branch", "mp"), 0),), GW)
    grid_height = grid_field.shape[0] // GW
    channels = grid_field.shape[1]
    shaped = extended.reshape(grid_height + 2, GW, channels)
    padded = jnp.pad(shaped, ((0, 0), (1, 1), (0, 0)))
    running_sum = jnp.zeros((grid_height * GW, kernel.shape[3]), jnp.float32)
    for row_off in range(3):
        for col_off in range(3):
            window = padded[row_off : row_off + grid_height, col_off : col_off + GW, :].reshape(
                -1, channels
            )
            running_sum = running_sum + jnp.dot(
                window, kernel[row_off, col_off], preferred_element_type=jnp.float32
            )
    return running_sum + bias_vec


def attend_piece(fold_state, piece_rows, first_row, query_heads, view_counts, tok_view, heads_dev):
    run_max, run_sum, run_acc = fold_state
    length = piece_rows.shape[0]
    head_width = heads_dev * HD
    score_scale = 1.0 / HD**0.5
    slot_range = jnp.arange(view_counts.shape[0], dtype=jnp.int32)
    for offset in range(0, length, KEY_BLOCK):
        block_size = min(KEY_BLOCK, length - offset)
        key_block = piece_rows[offset : offset + block_size]
        key_part = key_block[:, :head_width].reshape(block_size, heads_dev, HD)
        value_part = key_block[:, head_width:].reshape(block_size, heads_dev, HD)
        positions = first_row + offset + jnp.arange(block_size, dtype=jnp.int32)
        slot_view = positions // tok_view
        view_match = slot_view[:, None] == slot_range[None, :]
        view_limit = jnp.sum(jnp.where(view_match, view_counts[None, :], 0), axis=1)
        key_valid = positions % tok_view < view_limit
        scores = (
            jnp.einsum("qhd,khd->hqk", query_heads, key_part, preferred_element_type=jnp.float32)
            * score_scale
        )
        scores = jnp.where(key_valid[None, None, :], scores, NEG_FILL)
        new_max = jnp.maximum(run_max, jnp.max(scores, axis=2))
        weights = jnp.where(key_valid[None, None, :], jnp.exp(scores - new_max[:, :, None]), 0.0)
        rescale = jnp.exp(run_max - new_max)
        run_sum = run_sum * rescale + jnp.sum(weights, axis=2)
        run_acc = run_acc * rescale[:, :, None] + jnp.einsum(
            "hqk,khd->hqd",
            weights.astype(jnp.bfloat16),
            value_part,
            preferred_element_type=jnp.float32,
        )
        run_max = new_max
    return (run_max, run_sum, run_acc)


def select_rows(table_rows, wanted):
    row_total = table_rows.shape[0]
    inside = (wanted >= 0) & (wanted < row_total)
    picked = jnp.take(table_rows, jnp.clip(wanted, 0, row_total - 1), axis=0)
    return jnp.where(inside[:, None], picked, 0.0)


def local(
    tokens,
    view_table,
    view_ids,
    view_counts,
    norm_in_gain,
    in_weight,
    out_weight,
    norm_attn_gain,
    qkv_weight,
    head_gain,
    depth_weight,
    kernel_one,
    bias_one,
    kernel_two,
    bias_two,
    track_weight,
    track_ids,
):
    tok_view = tokens.shape[0]
    view_index = lax.axis_index("view")
    inner_index = lax.axis_index(("branch", "mp"))
    inner_count = lax.axis_size(("branch", "mp"))
    head_width = qkv_weight.shape[2]
    heads_dev = head_width // HD
    slot_match = jnp.arange(view_ids.shape[0], dtype=jnp.int32) == view_index
    my_view = jnp.sum(jnp.where(slot_match, view_ids, 0))
    my_count = jnp.sum(jnp.where(slot_match, view_counts, 0))
    table_pick = (jnp.arange(view_table.shape[0], dtype=jnp.int32) == my_view).astype(jnp.float32)
    view_embed = jnp.dot(
        table_pick, view_table.astype(jnp.float32), precision=lax.Precision.HIGHEST
    )
    residual_in = tokens.astype(jnp.float32) + view_embed[None, :]
    normed_in = layer_norm(residual_in, norm_in_gain).astype(jnp.bfloat16)
    hidden = jax.nn.gelu(
        jnp.dot(normed_in, in_weight, preferred_element_type=jnp.float32), approximate=True
    ).astype(jnp.bfloat16)
    share_rows = tok_view // inner_count
    row_block = hidden
    summed = lax.psum_scatter(
        jnp.dot(row_block, out_weight, preferred_element_type=jnp.float32),
        ("branch", "mp"),
        scatter_dimension=0,
        tiled=True,
    )
    own_residual = lax.dynamic_slice_in_dim(residual_in, inner_index * share_rows, share_rows, 0)
    mlp_out = (own_residual + summed).astype(jnp.bfloat16)
    normed_share = layer_norm(mlp_out.astype(jnp.float32), norm_attn_gain).astype(jnp.bfloat16)
    normed_attn = lax.all_gather(normed_share, ("branch", "mp"), axis=0, tiled=True)
    projected = jnp.dot(
        normed_attn,
        qkv_weight.reshape(qkv_weight.shape[0], 3 * head_width),
        preferred_element_type=jnp.float32,
    )
    query_heads = head_norm(
        projected[:, :head_width].reshape(tok_view, heads_dev, HD), head_gain[0]
    ).astype(jnp.bfloat16)
    key_heads = head_norm(
        projected[:, head_width : 2 * head_width].reshape(tok_view, heads_dev, HD), head_gain[1]
    ).astype(jnp.bfloat16)
    value_heads = projected[:, 2 * head_width :].astype(jnp.bfloat16)
    stacked = jnp.concatenate([key_heads.reshape(tok_view, head_width), value_heads], axis=1)
    fold_start = (
        jnp.full((heads_dev, tok_view), NEG_FILL, jnp.float32),
        jnp.zeros((heads_dev, tok_view), jnp.float32),
        jnp.zeros((heads_dev, tok_view, HD), jnp.float32),
    )
    run_max, run_sum, run_acc = attend_piece(
        fold_start,
        lax.all_gather(stacked, "view", axis=0, tiled=True),
        jnp.int32(0),
        query_heads,
        view_counts,
        tok_view,
        heads_dev,
    )
    attended = (
        (run_acc / run_sum[:, :, None])
        .astype(jnp.bfloat16)
        .transpose(1, 0, 2)
        .reshape(tok_view, head_width)
    )
    depth_rows = tok_view // inner_count
    row_pos = inner_index * depth_rows + jnp.arange(depth_rows, dtype=jnp.int32)
    row_valid = (row_pos < my_count).astype(jnp.float32)[:, None]
    row_block = attended
    depth_sum = lax.psum_scatter(
        jnp.dot(row_block, depth_weight, preferred_element_type=jnp.float32).astype(jnp.bfloat16),
        ("branch", "mp"),
        scatter_dimension=0,
        tiled=True,
    ).astype(jnp.float32)
    track_proj = jnp.dot(attended, track_weight, preferred_element_type=jnp.float32)
    wanted = track_ids - view_index * tok_view
    track_out = lax.psum_scatter(
        select_rows(track_proj, wanted), ("view", "branch", "mp"), scatter_dimension=0, tiled=True
    )
    features = (depth_sum * row_valid).astype(jnp.bfloat16)
    first_conv = jnp.maximum(conv_rows(features, kernel_one, bias_one), 0.0).astype(jnp.bfloat16)
    depth_out = conv_rows(first_conv, kernel_two, bias_two).astype(jnp.bfloat16)
    return (depth_out, track_out)


def xor_pairs(size, step):
    return [(i, i ^ step) for i in range(size)]


def peers(value, axis, size):
    return [lax.ppermute(value, axis, xor_pairs(size, k)) for k in range(1, size)]


def shift_cols(rows, col_off):
    height = rows.shape[0] // GW
    shaped = jnp.pad(rows.reshape(height, GW, -1), ((0, 0), (1, 1), (0, 0)))
    return shaped[:, col_off : col_off + GW, :].reshape(rows.shape)


def conv_valid(rows, kernel, bias_vec):
    out_rows = rows.shape[0] - 2 * GW
    total = bias_vec[None, :] + jnp.zeros((out_rows, kernel.shape[3]), jnp.float32)
    for col_off in range(3):
        shifted = shift_cols(rows, col_off)
        for row_off in range(3):
            total = total + jnp.dot(
                shifted[row_off * GW : row_off * GW + out_rows],
                kernel[row_off, col_off],
                preferred_element_type=jnp.float32,
            )
    return total


def local_fast(
    tokens,
    view_table,
    view_ids,
    view_counts,
    norm_in_gain,
    in_weight,
    out_weight,
    norm_attn_gain,
    qkv_weight,
    head_gain,
    depth_weight,
    kernel_one,
    bias_one,
    kernel_two,
    bias_two,
    track_weight,
    track_ids,
):
    tok_view = tokens.shape[0]
    views = lax.axis_size("view")
    branches, cores = lax.axis_size("branch"), lax.axis_size("mp")
    inner_axes = ("branch", "mp")
    inner_count = branches * cores
    view_index = lax.axis_index("view")
    inner_index = lax.axis_index(inner_axes)
    head_width = qkv_weight.shape[2]
    heads_dev = head_width // HD
    share = tok_view // inner_count
    my_view = view_ids[view_index]
    view_embed = view_table[my_view].astype(jnp.float32)
    residual_in = tokens.astype(jnp.float32) + view_embed[None, :]
    normed_in = layer_norm(residual_in, norm_in_gain).astype(jnp.bfloat16)
    hidden = jax.nn.gelu(
        jnp.dot(normed_in, in_weight, preferred_element_type=jnp.float32), approximate=True
    ).astype(jnp.bfloat16)
    part = jnp.dot(hidden, out_weight, preferred_element_type=jnp.float32)
    for axis, size in (("mp", cores), ("branch", branches)):
        sent = part.astype(jnp.bfloat16)
        part = sent.astype(jnp.float32)
        for got in peers(sent, axis, size):
            part = part + got.astype(jnp.float32)
    mlp_out = (residual_in + part).astype(jnp.bfloat16)
    normed_attn = layer_norm(mlp_out.astype(jnp.float32), norm_attn_gain).astype(jnp.bfloat16)
    projected = jnp.dot(
        normed_attn,
        qkv_weight.reshape(qkv_weight.shape[0], 3 * head_width),
        preferred_element_type=jnp.float32,
    )
    queries = (
        head_norm(projected[:, :head_width].reshape(tok_view, heads_dev, HD), head_gain[0])
        .astype(jnp.bfloat16)
        .reshape(tok_view, head_width)
    )
    keys = (
        head_norm(
            projected[:, head_width : 2 * head_width].reshape(tok_view, heads_dev, HD), head_gain[1]
        )
        .astype(jnp.bfloat16)
        .reshape(tok_view, head_width)
    )
    values = projected[:, 2 * head_width :].astype(jnp.bfloat16)
    stacked = jnp.concatenate([keys, values], axis=1)
    asked = track_ids.shape[0] // views
    wanted = track_ids - view_index * tok_view
    pick = (wanted[:, None] == jnp.arange(tok_view, dtype=jnp.int32)[None, :]).astype(jnp.bfloat16)
    picked = jnp.dot(pick, queries, preferred_element_type=jnp.float32).astype(jnp.bfloat16)
    half = asked // 2

    def message(k):
        mine = lax.dynamic_slice_in_dim(picked, (view_index ^ k) * asked, asked, 0)
        mine = jnp.concatenate([mine[:half], mine[half:]], axis=1)
        return jnp.concatenate([stacked, mine], axis=0)

    blocks = [message(0)] + [
        lax.ppermute(message(k), "view", xor_pairs(views, k)) for k in range(1, views)
    ]
    asked_rows = blocks[0][tok_view:].astype(jnp.float32)
    for block in blocks[1:]:
        asked_rows = asked_rows + block[tok_view:].astype(jnp.float32)
    asked_rows = asked_rows.astype(jnp.bfloat16)
    asked_rows = jnp.concatenate([asked_rows[:, :head_width], asked_rows[:, head_width:]], axis=0)
    all_queries = jnp.concatenate([queries, asked_rows], axis=0).reshape(-1, heads_dev, HD)
    score_scale = 1.0 / HD**0.5
    scores = []
    for k, block in enumerate(blocks):
        part_keys = block[:tok_view, :head_width].reshape(tok_view, heads_dev, HD)
        valid = jnp.arange(tok_view, dtype=jnp.int32) < view_counts[view_index ^ k]
        score = (
            jnp.einsum("qhd,khd->hqk", all_queries, part_keys, preferred_element_type=jnp.float32)
            * score_scale
        )
        scores.append(jnp.where(valid[None, None, :], score, NEG_FILL))
    scores = jnp.concatenate(scores, axis=2)
    row_max = jnp.max(scores, axis=2, keepdims=True)
    weights = jnp.exp(scores - row_max)
    row_sum = jnp.sum(weights, axis=2, keepdims=True)
    all_values = jnp.concatenate([block[:tok_view, head_width:] for block in blocks], axis=0)
    mixed = jnp.einsum(
        "hqk,khd->hqd",
        weights.astype(jnp.bfloat16),
        all_values.reshape(-1, heads_dev, HD),
        preferred_element_type=jnp.float32,
    )
    attended = (mixed / row_sum).astype(jnp.bfloat16).transpose(1, 0, 2).reshape(-1, head_width)
    depth_part = jnp.dot(
        attended[:tok_view], depth_weight, preferred_element_type=jnp.float32
    ).astype(jnp.bfloat16)
    track_part = jnp.dot(
        attended[tok_view:], track_weight, preferred_element_type=jnp.float32
    ).astype(jnp.bfloat16)
    own = asked // inner_count
    depth_sum = depth_part.astype(jnp.float32)
    track_sum = lax.dynamic_slice_in_dim(track_part, inner_index * own, own, 0).astype(jnp.float32)
    for k in range(1, inner_count):
        rows = lax.dynamic_slice_in_dim(track_part, (inner_index ^ k) * own, own, 0)
        rows = jnp.pad(rows, ((0, 0), (0, depth_part.shape[1] - rows.shape[1])))
        got = lax.ppermute(
            jnp.concatenate([depth_part, rows], axis=0), inner_axes, xor_pairs(inner_count, k)
        ).astype(jnp.float32)
        depth_sum = depth_sum + got[:tok_view]
        track_sum = track_sum + got[tok_view:, : track_part.shape[1]]
    my_count = view_counts[view_index]
    row_valid = (jnp.arange(tok_view, dtype=jnp.int32) < my_count).astype(jnp.float32)[:, None]
    features = (depth_sum * row_valid).astype(jnp.bfloat16)
    near = share + 4 * GW
    padded = jnp.pad(features, ((2 * GW, 2 * GW), (0, 0)))
    window = lax.dynamic_slice_in_dim(padded, inner_index * share, near, 0)
    first = jnp.maximum(conv_valid(window, kernel_one, bias_one), 0.0)
    place = inner_index * share - GW + jnp.arange(near - 2 * GW, dtype=jnp.int32)
    inside = (place >= 0) & (place < tok_view)
    first = jnp.where(inside[:, None], first, 0.0).astype(jnp.bfloat16)
    depth_out = conv_valid(first, kernel_two, bias_two).astype(jnp.bfloat16)
    return (depth_out, track_sum)


def power_of_two(size):
    return size & (size - 1) == 0


def pick_path(*args):
    tok_view, head_width = args[0].shape[0], args[8].shape[2]
    sizes = [lax.axis_size(axis) for axis in ("view", "branch", "mp")]
    inner_count = sizes[1] * sizes[2]
    share = tok_view // inner_count
    fits = all(power_of_two(size) for size in sizes) and share % GW == 0
    fits = fits and head_width % 128 == 0 and (args[16].shape[0] // sizes[0]) % inner_count == 0
    return local_fast(*args) if fits else local(*args)


def solution(mesh):
    in_specs = (
        P(("groups", "view"), None),
        P(),
        P("groups"),
        P("groups"),
        P(),
        P(None, ("branch", "mp")),
        P(("branch", "mp"), None),
        P(),
        P(None, None, ("branch", "mp")),
        P(),
        P(("branch", "mp"), None),
        P(),
        P(),
        P(),
        P(),
        P(("branch", "mp"), None),
        P("groups"),
    )
    out_specs = (
        P(("groups", "view", "branch", "mp"), None),
        P(("groups", "view", "branch", "mp"), None),
    )
    return jax.shard_map(pick_path, mesh=mesh, in_specs=in_specs, out_specs=out_specs, check_vma=False)
```

```python
import functools

import jax
import jax.numpy as jnp
from jax import lax
from jax.experimental import pallas as pl
from jax.experimental.pallas import tpu as pltpu
from jax.sharding import PartitionSpec as P

HD = 64
GW = 32


EPS_NORM = 1e-05
EPS_HEAD = 1e-06
NEG_FILL = -1e30
KEY_BLOCK = 1024


def with_halo(value, sides, width):
    for axis, dim in sides:
        size, length = (lax.axis_size(axis), value.shape[dim])
        up = [(i, (i + 1) % size) for i in range(size - 1)]
        down = [(j, i) for i, j in up]
        last = lax.slice_in_dim(value, length - width, length, axis=dim)
        first = lax.slice_in_dim(value, 0, width, axis=dim)
        before = lax.ppermute(last, axis, up)
        after = lax.ppermute(first, axis, down)
        value = jnp.concatenate([before, value, after], axis=dim)
    return value


def layer_norm(values, gain_vec):
    row_mean = jnp.mean(values, axis=-1, keepdims=True)
    centered = values - row_mean
    row_var = jnp.mean(centered * centered, axis=-1, keepdims=True)
    return centered * lax.rsqrt(row_var + EPS_NORM) * gain_vec


def head_norm(values, gain_vec):
    head_mean = jnp.mean(values, axis=-1, keepdims=True)
    centered = values - head_mean
    head_var = jnp.mean(centered * centered, axis=-1, keepdims=True)
    return centered * lax.rsqrt(head_var + EPS_HEAD) * gain_vec


def conv_rows(grid_field, kernel, bias_vec):
    extended = with_halo(grid_field, ((("branch", "mp"), 0),), GW)
    grid_height = grid_field.shape[0] // GW
    channels = grid_field.shape[1]
    shaped = extended.reshape(grid_height + 2, GW, channels)
    padded = jnp.pad(shaped, ((0, 0), (1, 1), (0, 0)))
    running_sum = jnp.zeros((grid_height * GW, kernel.shape[3]), jnp.float32)
    for row_off in range(3):
        for col_off in range(3):
            window = padded[row_off : row_off + grid_height, col_off : col_off + GW, :].reshape(
                -1, channels
            )
            running_sum = running_sum + jnp.dot(
                window, kernel[row_off, col_off], preferred_element_type=jnp.float32
            )
    return running_sum + bias_vec


def attend_piece(fold_state, piece_rows, first_row, query_heads, view_counts, tok_view, heads_dev):
    run_max, run_sum, run_acc = fold_state
    length = piece_rows.shape[0]
    head_width = heads_dev * HD
    score_scale = 1.0 / HD**0.5
    slot_range = jnp.arange(view_counts.shape[0], dtype=jnp.int32)
    for offset in range(0, length, KEY_BLOCK):
        block_size = min(KEY_BLOCK, length - offset)
        key_block = piece_rows[offset : offset + block_size]
        key_part = key_block[:, :head_width].reshape(block_size, heads_dev, HD)
        value_part = key_block[:, head_width:].reshape(block_size, heads_dev, HD)
        positions = first_row + offset + jnp.arange(block_size, dtype=jnp.int32)
        slot_view = positions // tok_view
        view_match = slot_view[:, None] == slot_range[None, :]
        view_limit = jnp.sum(jnp.where(view_match, view_counts[None, :], 0), axis=1)
        key_valid = positions % tok_view < view_limit
        scores = (
            jnp.einsum("qhd,khd->hqk", query_heads, key_part, preferred_element_type=jnp.float32)
            * score_scale
        )
        scores = jnp.where(key_valid[None, None, :], scores, NEG_FILL)
        new_max = jnp.maximum(run_max, jnp.max(scores, axis=2))
        weights = jnp.where(key_valid[None, None, :], jnp.exp(scores - new_max[:, :, None]), 0.0)
        rescale = jnp.exp(run_max - new_max)
        run_sum = run_sum * rescale + jnp.sum(weights, axis=2)
        run_acc = run_acc * rescale[:, :, None] + jnp.einsum(
            "hqk,khd->hqd",
            weights.astype(jnp.bfloat16),
            value_part,
            preferred_element_type=jnp.float32,
        )
        run_max = new_max
    return (run_max, run_sum, run_acc)


def select_rows(table_rows, wanted):
    row_total = table_rows.shape[0]
    inside = (wanted >= 0) & (wanted < row_total)
    picked = jnp.take(table_rows, jnp.clip(wanted, 0, row_total - 1), axis=0)
    return jnp.where(inside[:, None], picked, 0.0)


def local(
    tokens,
    view_table,
    view_ids,
    view_counts,
    norm_in_gain,
    in_weight,
    out_weight,
    norm_attn_gain,
    qkv_weight,
    head_gain,
    depth_weight,
    kernel_one,
    bias_one,
    kernel_two,
    bias_two,
    track_weight,
    track_ids,
):
    tok_view = tokens.shape[0]
    view_index = lax.axis_index("view")
    inner_index = lax.axis_index(("branch", "mp"))
    inner_count = lax.axis_size(("branch", "mp"))
    head_width = qkv_weight.shape[2]
    heads_dev = head_width // HD
    slot_match = jnp.arange(view_ids.shape[0], dtype=jnp.int32) == view_index
    my_view = jnp.sum(jnp.where(slot_match, view_ids, 0))
    my_count = jnp.sum(jnp.where(slot_match, view_counts, 0))
    table_pick = (jnp.arange(view_table.shape[0], dtype=jnp.int32) == my_view).astype(jnp.float32)
    view_embed = jnp.dot(
        table_pick, view_table.astype(jnp.float32), precision=lax.Precision.HIGHEST
    )
    residual_in = tokens.astype(jnp.float32) + view_embed[None, :]
    normed_in = layer_norm(residual_in, norm_in_gain).astype(jnp.bfloat16)
    hidden = jax.nn.gelu(
        jnp.dot(normed_in, in_weight, preferred_element_type=jnp.float32), approximate=True
    ).astype(jnp.bfloat16)
    share_rows = tok_view // inner_count
    row_block = hidden
    summed = lax.psum_scatter(
        jnp.dot(row_block, out_weight, preferred_element_type=jnp.float32),
        ("branch", "mp"),
        scatter_dimension=0,
        tiled=True,
    )
    own_residual = lax.dynamic_slice_in_dim(residual_in, inner_index * share_rows, share_rows, 0)
    mlp_out = (own_residual + summed).astype(jnp.bfloat16)
    normed_share = layer_norm(mlp_out.astype(jnp.float32), norm_attn_gain).astype(jnp.bfloat16)
    normed_attn = lax.all_gather(normed_share, ("branch", "mp"), axis=0, tiled=True)
    projected = jnp.dot(
        normed_attn,
        qkv_weight.reshape(qkv_weight.shape[0], 3 * head_width),
        preferred_element_type=jnp.float32,
    )
    query_heads = head_norm(
        projected[:, :head_width].reshape(tok_view, heads_dev, HD), head_gain[0]
    ).astype(jnp.bfloat16)
    key_heads = head_norm(
        projected[:, head_width : 2 * head_width].reshape(tok_view, heads_dev, HD), head_gain[1]
    ).astype(jnp.bfloat16)
    value_heads = projected[:, 2 * head_width :].astype(jnp.bfloat16)
    stacked = jnp.concatenate([key_heads.reshape(tok_view, head_width), value_heads], axis=1)
    fold_start = (
        jnp.full((heads_dev, tok_view), NEG_FILL, jnp.float32),
        jnp.zeros((heads_dev, tok_view), jnp.float32),
        jnp.zeros((heads_dev, tok_view, HD), jnp.float32),
    )
    run_max, run_sum, run_acc = attend_piece(
        fold_start,
        lax.all_gather(stacked, "view", axis=0, tiled=True),
        jnp.int32(0),
        query_heads,
        view_counts,
        tok_view,
        heads_dev,
    )
    attended = (
        (run_acc / run_sum[:, :, None])
        .astype(jnp.bfloat16)
        .transpose(1, 0, 2)
        .reshape(tok_view, head_width)
    )
    depth_rows = tok_view // inner_count
    row_pos = inner_index * depth_rows + jnp.arange(depth_rows, dtype=jnp.int32)
    row_valid = (row_pos < my_count).astype(jnp.float32)[:, None]
    row_block = attended
    depth_sum = lax.psum_scatter(
        jnp.dot(row_block, depth_weight, preferred_element_type=jnp.float32).astype(jnp.bfloat16),
        ("branch", "mp"),
        scatter_dimension=0,
        tiled=True,
    ).astype(jnp.float32)
    track_proj = jnp.dot(attended, track_weight, preferred_element_type=jnp.float32)
    wanted = track_ids - view_index * tok_view
    track_out = lax.psum_scatter(
        select_rows(track_proj, wanted), ("view", "branch", "mp"), scatter_dimension=0, tiled=True
    )
    features = (depth_sum * row_valid).astype(jnp.bfloat16)
    first_conv = jnp.maximum(conv_rows(features, kernel_one, bias_one), 0.0).astype(jnp.bfloat16)
    depth_out = conv_rows(first_conv, kernel_two, bias_two).astype(jnp.bfloat16)
    return (depth_out, track_out)


VMEM = pl.BlockSpec(memory_space=pltpu.VMEM)
SMEM = pl.BlockSpec(memory_space=pltpu.SMEM)
COLUMNS = 256
VMEM_GRANT = 16 << 20
OPEN_GRANT = 1 << 20


def dot(left, right):
    return jnp.dot(left, right, preferred_element_type=jnp.float32)


def run_kernel(body, out_shape, in_specs, scratch=(), grant=VMEM_GRANT, cost=None):
    return pl.pallas_call(
        body,
        out_shape=out_shape,
        in_specs=in_specs,
        out_specs=jax.tree.map(lambda _: VMEM, out_shape),
        scratch_shapes=list(scratch),
        compiler_params=pltpu.CompilerParams(vmem_limit_bytes=grant),
        cost_estimate=cost,
    )


def xor_pairs(size, step):
    return [(i, i ^ step) for i in range(size)]


def peers(value, axis, size):
    return [lax.ppermute(value, axis, xor_pairs(size, k)) for k in range(1, size)]


def column_blocks(width):
    return [slice(low, min(low + COLUMNS, width)) for low in range(0, width, COLUMNS)]


def open_kernel(out_ref):
    out_ref[...] = jnp.zeros(out_ref.shape, out_ref.dtype)


def mlp_kernel(
    ids_ref, table_ref, tokens_ref, gain_ref, in_ref, out_ref, open_ref, part_ref, embed_ref, hidden_ref
):
    my_view = ids_ref[lax.axis_index("view")]
    row = lax.broadcasted_iota(jnp.int32, table_ref.shape, 0)
    table = table_ref[...].astype(jnp.float32)
    embed_ref[...] = jnp.sum(jnp.where(row == my_view, table, 0.0), axis=0, keepdims=True)
    residual = tokens_ref[...].astype(jnp.float32) + embed_ref[...]
    normed = layer_norm(residual, gain_ref[...]).astype(jnp.bfloat16)
    for cols in column_blocks(in_ref.shape[1]):
        hidden_ref[:, cols] = jax.nn.gelu(dot(normed, in_ref[:, cols]), approximate=True).astype(
            jnp.bfloat16
        )
    hidden = hidden_ref[...]
    for cols in column_blocks(out_ref.shape[1]):
        part_ref[:, cols] = dot(hidden, out_ref[:, cols]).astype(jnp.bfloat16)


def split_dot(values, mixer):
    high = values.astype(jnp.bfloat16)
    rest = values - high.astype(jnp.float32)
    middle = rest.astype(jnp.bfloat16)
    low = (rest - middle.astype(jnp.float32)).astype(jnp.bfloat16)
    return dot(high, mixer) + dot(middle, mixer) + dot(low, mixer)


def norm_heads(values, gain):
    width = values.shape[1]
    row = lax.broadcasted_iota(jnp.int32, (width, width), 0) // HD
    col = lax.broadcasted_iota(jnp.int32, (width, width), 1) // HD
    mixer = jnp.where(row == col, 1.0 / HD, 0.0).astype(jnp.bfloat16)
    centered = values - split_dot(values, mixer)
    spread = split_dot(centered * centered, mixer)
    return (centered * lax.rsqrt(spread + EPS_HEAD) * gain).astype(jnp.bfloat16)


def project_kernel(
    embed_ref,
    tokens_ref,
    *refs,
    sums,
    views,
):
    sum_refs, refs = refs[:sums], refs[sums:]
    gain_ref, qkv_ref, head_gain_ref, track_ref = refs[:4]
    query_ref, message_refs, picked_ref = refs[4], refs[5 : 5 + views], refs[5 + views]
    tok_view, width = query_ref.shape
    total = tokens_ref[...].astype(jnp.float32) + embed_ref[...]
    for ref in sum_refs:
        total = total + ref[...].astype(jnp.float32)
    mlp_out = total.astype(jnp.bfloat16).astype(jnp.float32)
    normed = layer_norm(mlp_out, gain_ref[...]).astype(jnp.bfloat16)
    keys = norm_heads(dot(normed, qkv_ref[1]), head_gain_ref[1:2, :])
    values = dot(normed, qkv_ref[2]).astype(jnp.bfloat16)
    queries = norm_heads(dot(normed, qkv_ref[0]), head_gain_ref[0:1, :])
    query_ref[...] = queries
    view_index = lax.axis_index("view")
    place = lax.broadcasted_iota(jnp.int32, (tok_view, track_ref.shape[1]), 0)
    wanted = track_ref[...] - view_index * tok_view
    chosen = jnp.where(place == wanted, 1.0, 0.0).astype(jnp.bfloat16)
    picked_ref[...] = lax.dot_general(
        chosen, queries, (((0,), (0,)), ((), ())), preferred_element_type=jnp.float32
    ).astype(jnp.bfloat16)
    asked = track_ref.shape[1] // views
    half = asked // 2
    for k in range(views):
        ref = message_refs[k]
        start = pl.multiple_of((view_index ^ k) * asked, asked)
        mine = picked_ref[pl.ds(start, asked), :]
        ref[:tok_view, :width] = keys
        ref[:tok_view, width:] = values
        ref[tok_view:, :width] = mine[:half]
        ref[tok_view:, width:] = mine[half:]


def attend_kernel(counts_ref, query_ref, *refs, views, inner_count):
    block_refs, refs = refs[:views], refs[views:]
    depth_ref, track_ref = refs[:2]
    message_refs, attended_ref, part_ref = (
        refs[2 : 2 + inner_count],
        refs[2 + inner_count],
        refs[3 + inner_count],
    )
    tok_view, width = query_ref.shape
    half = block_refs[0].shape[0] - tok_view
    view_index = lax.axis_index("view")
    asked_rows = block_refs[0][tok_view:, :].astype(jnp.float32)
    for ref in block_refs[1:]:
        asked_rows = asked_rows + ref[tok_view:, :].astype(jnp.float32)
    asked_rows = asked_rows.astype(jnp.bfloat16)
    queries = jnp.concatenate(
        [query_ref[...], asked_rows[:, :width], asked_rows[:, width:]], axis=0
    )
    rows = queries.shape[0]
    key_place = lax.broadcasted_iota(jnp.int32, (rows, tok_view), 1)
    valid = [key_place < counts_ref[view_index ^ k] for k in range(views)]
    lane = lax.broadcasted_iota(jnp.int32, (rows, 128), 1)
    score_scale = 1.0 / HD**0.5
    for low in range(0, width, 128):
        tile = queries[:, low : low + 128]
        mixed = []
        for first in range(0, 128, HD):
            mine = (lane >= first) & (lane < first + HD)
            head = jnp.where(mine, tile, jnp.zeros_like(tile))
            scores = []
            for k, ref in enumerate(block_refs):
                keys = ref[:tok_view, low : low + 128]
                score = lax.dot_general(
                    head, keys, (((1,), (1,)), ((), ())), preferred_element_type=jnp.float32
                )
                scores.append(jnp.where(valid[k], score * score_scale, NEG_FILL))
            row_max = functools.reduce(jnp.maximum, scores).max(axis=1, keepdims=True)
            weights = [jnp.exp(score - row_max) for score in scores]
            row_sum = functools.reduce(jnp.add, weights).sum(axis=1, keepdims=True)
            total = None
            for k, ref in enumerate(block_refs):
                values = ref[:tok_view, width + low : width + low + 128]
                term = dot(weights[k].astype(jnp.bfloat16), values)
                total = term if total is None else total + term
            mixed.append((mine, total / row_sum))
        result = mixed[0][1]
        for mine, value in mixed[1:]:
            result = jnp.where(mine, value, result)
        attended_ref[:, low : low + 128] = result.astype(jnp.bfloat16)
    depth = dot(attended_ref[:tok_view, :], depth_ref[...]).astype(jnp.bfloat16)
    part_ref[...] = dot(attended_ref[tok_view:, :], track_ref[...])
    own = part_ref.shape[0] // inner_count
    inner_index = lax.axis_index(("branch", "mp"))
    track_width = part_ref.shape[1]
    for k, ref in enumerate(message_refs):
        start = pl.multiple_of((inner_index ^ k) * own, own)
        ref[:tok_view, :] = depth
        ref[tok_view:, :track_width] = part_ref[pl.ds(start, own), :].astype(jnp.bfloat16)
        ref[tok_view:, track_width:] = jnp.zeros(
            (own, ref.shape[1] - track_width), jnp.bfloat16
        )


def beside(rows):
    length = rows.shape[0]
    col = lax.broadcasted_iota(jnp.int32, rows.shape, 0) % GW
    before = jnp.where(col == 0, 0.0, pltpu.roll(rows, 1, 0))
    after = jnp.where(col == GW - 1, 0.0, pltpu.roll(rows, length - 1, 0))
    return jnp.concatenate([before, rows, after], axis=1).astype(jnp.bfloat16)


def conv_taps(rows, kernel_ref, bias_ref):
    wide = beside(rows)
    out_rows = rows.shape[0] - 2 * GW
    total = dot(wide[:out_rows], kernel_ref[0])
    for row_off in range(1, 3):
        total = total + dot(wide[row_off * GW : row_off * GW + out_rows], kernel_ref[row_off])
    return total + bias_ref[...]


def conv_kernel(counts_ref, *refs, inner_count):
    message_refs, refs = refs[:inner_count], refs[inner_count:]
    one_ref, bias_one_ref, two_ref, bias_two_ref, depth_ref, track_ref, feature_ref = refs
    tok_view = feature_ref.shape[0] - 4 * GW
    share = depth_ref.shape[0]
    total = message_refs[0][...].astype(jnp.float32)
    for ref in message_refs[1:]:
        total = total + ref[...].astype(jnp.float32)
    track_ref[...] = total[tok_view:, : track_ref.shape[1]]
    my_count = counts_ref[lax.axis_index("view")]
    place = lax.broadcasted_iota(jnp.int32, (tok_view, total.shape[1]), 0)
    row_valid = jnp.where(place < my_count, 1.0, 0.0)
    edge = jnp.zeros((2 * GW, total.shape[1]), jnp.float32)
    feature_ref[: 2 * GW, :] = edge
    feature_ref[2 * GW + tok_view :, :] = edge
    features = (total[:tok_view] * row_valid).astype(jnp.bfloat16)
    feature_ref[2 * GW : 2 * GW + tok_view, :] = features.astype(jnp.float32)
    begin = lax.axis_index(("branch", "mp")) * share
    near = share + 4 * GW
    window = feature_ref[pl.ds(pl.multiple_of(begin, GW), near), :]
    first = jnp.maximum(conv_taps(window, one_ref, bias_one_ref), 0.0)
    at = lax.broadcasted_iota(jnp.int32, first.shape, 0) + (begin - GW)
    first = jnp.where((at >= 0) & (at < tok_view), first, 0.0)
    first = first.astype(jnp.bfloat16).astype(jnp.float32)
    depth_ref[...] = conv_taps(first, two_ref, bias_two_ref).astype(depth_ref.dtype)


def local_fast(
    tokens,
    view_table,
    view_ids,
    view_counts,
    norm_in_gain,
    in_weight,
    out_weight,
    norm_attn_gain,
    qkv_weight,
    head_gain,
    depth_weight,
    kernel_one,
    bias_one,
    kernel_two,
    bias_two,
    track_weight,
    track_ids,
):
    shape = jax.ShapeDtypeStruct
    tok_view, width = tokens.shape
    views = lax.axis_size("view")
    branches, cores = lax.axis_size("branch"), lax.axis_size("mp")
    inner_axes = ("branch", "mp")
    inner_count = branches * cores
    head_width = qkv_weight.shape[2]
    heads_dev = head_width // HD
    share = tok_view // inner_count
    hidden_units = in_weight.shape[1]
    channels = depth_weight.shape[1]
    opened = run_kernel(open_kernel, shape((8, 128), jnp.float32), [], (), OPEN_GRANT, pl.CostEstimate(flops=1 << 31, bytes_accessed=16 << 20, transcendentals=0))()
    part, embed = run_kernel(
        mlp_kernel,
        [shape((tok_view, width), jnp.bfloat16), shape((1, width), jnp.float32)],
        [SMEM] + [VMEM] * 6,
        [pltpu.VMEM((tok_view, hidden_units), jnp.bfloat16)],
    )(view_ids, view_table, tokens, norm_in_gain.reshape(1, -1), in_weight, out_weight, opened)
    chip = part.astype(jnp.float32)
    for got in peers(part, "mp", cores):
        chip = chip + got.astype(jnp.float32)
    chip = chip.astype(jnp.bfloat16)
    sums = [chip] + peers(chip, "branch", branches)
    asked = track_ids.shape[0] // views
    message = shape((tok_view + asked // 2, 2 * head_width), jnp.bfloat16)
    query, *blocks = run_kernel(
        functools.partial(project_kernel, sums=len(sums), views=views),
        [shape((tok_view, head_width), jnp.bfloat16)] + [message] * views,
        [VMEM] * (len(sums) + 6),
        [pltpu.VMEM((track_ids.shape[0], head_width), jnp.bfloat16)],
    )(
        embed,
        tokens,
        *sums,
        norm_attn_gain.reshape(1, -1),
        qkv_weight.transpose(1, 0, 2),
        jnp.tile(head_gain, (1, heads_dev)),
        track_ids.reshape(1, -1),
    )
    blocks = blocks[:1] + [
        lax.ppermute(blocks[k], "view", xor_pairs(views, k)) for k in range(1, views)
    ]
    track_width = track_weight.shape[1]
    own = asked // inner_count
    message = shape((tok_view + own, channels), jnp.bfloat16)
    pieces = run_kernel(
        functools.partial(attend_kernel, views=views, inner_count=inner_count),
        [message] * inner_count,
        [SMEM] + [VMEM] * (views + 3),
        [
            pltpu.VMEM((tok_view + asked, head_width), jnp.bfloat16),
            pltpu.VMEM((asked, track_width), jnp.float32),
        ],
    )(view_counts, query, *blocks, depth_weight, track_weight)
    pieces = [pieces[0]] + [
        lax.ppermute(pieces[k], inner_axes, xor_pairs(inner_count, k))
        for k in range(1, inner_count)
    ]
    return run_kernel(
        functools.partial(conv_kernel, inner_count=inner_count),
        [shape((share, channels), jnp.bfloat16), shape((own, track_width), jnp.float32)],
        [SMEM] + [VMEM] * (inner_count + 4),
        [pltpu.VMEM((tok_view + 4 * GW, channels), jnp.float32)],
    )(
        view_counts,
        *pieces,
        kernel_one.reshape(3, 3 * channels, channels),
        bias_one.reshape(1, -1),
        kernel_two.reshape(3, 3 * channels, channels),
        bias_two.reshape(1, -1),
    )


def power_of_two(size):
    return size & (size - 1) == 0


def pick_path(*args):
    tok_view, head_width = args[0].shape[0], args[8].shape[2]
    sizes = [lax.axis_size(axis) for axis in ("view", "branch", "mp")]
    inner_count = sizes[1] * sizes[2]
    share = tok_view // inner_count
    fits = all(power_of_two(size) for size in sizes) and share % GW == 0
    fits = fits and head_width % 128 == 0 and (args[16].shape[0] // sizes[0]) % inner_count == 0
    return local_fast(*args) if fits else local(*args)


def solution(mesh):
    in_specs = (
        P(("groups", "view"), None),
        P(),
        P("groups"),
        P("groups"),
        P(),
        P(None, ("branch", "mp")),
        P(("branch", "mp"), None),
        P(),
        P(None, None, ("branch", "mp")),
        P(),
        P(("branch", "mp"), None),
        P(),
        P(),
        P(),
        P(),
        P(("branch", "mp"), None),
        P("groups"),
    )
    out_specs = (
        P(("groups", "view", "branch", "mp"), None),
        P(("groups", "view", "branch", "mp"), None),
    )
    return jax.shard_map(pick_path, mesh=mesh, in_specs=in_specs, out_specs=out_specs, check_vma=False)
```
